128 devices in a mesh: row: 8 (over z_hi, x), sub: 16 (over z_lo, y, core).
Axes of the slice: x: 4, y: 4, z: 4 (z_hi: 2, z_lo: 2; z = z_hi * 2 + z_lo), core: 2. Of those that a mesh axis runs over, the one named last changes fastest.
Arguments:
- ritz_coefficients: bfloat16 [16384, 2048], P('row', 'sub'), may hold values from -6 to 6
- mode_map: int32 [128, 128], P(('row', 'sub')), may hold values from 0 to 127, each once within a row
- leaf_count: int32 [128], P(('row', 'sub')), may hold values from 24 to 48, as said below
- mode_blocks: bfloat16 [133120, 2048], P(('row', 'sub'))
Outputs:
- eigenvectors: bfloat16 [262144, 2048], P(('row', 'sub'))
The draws below stay inside these ranges and needn't reach their ends.
Inputs may be any that keep to these rules, and one draw needn't show every extreme that they name: `mode_map`: each row is a permutation of 0 to 127. `leaf_count`: some substructure uses all 48 interior modes.
All inputs are finite; a program needn't handle non-finite values.
Results may differ from the reference program's by a relative error of at most 0.001.
Values may be sent and summed in bfloat16 or wider, within the bound.
No kernel may reach another device: no remote copies, remote signals or barrier semaphores. Data moves between devices by JAX's collectives and lax.ppermute only.
A program may use at most 64 MiB of HBM per device.

```python
import jax
import jax.numpy as jnp
from jax import lax

NEV = 2048
KM = 128
SR = 16
LEVELS = 5
NDOF = 2048
LM = 48
MCOLS = 1040
NSUBS = 128
K = 16384


def draw_leaf_count(key, part):
    counts = jax.random.randint(key, (NSUBS,), LM // 2, LM + 1)
    position = jax.random.randint(jax.random.fold_in(key, 7), (), 0, NSUBS)
    return counts.at[position].set(LM).astype(jnp.int32)


def draw_mode_blocks(key, part):
    total_rows = NSUBS * MCOLS
    column = jnp.arange(total_rows, dtype=jnp.int32) % MCOLS
    offset = column - LM
    level_number = jnp.ones_like(offset)
    for extra in range(2, LEVELS + 1):
        level_number = level_number + (offset >= SR * (2 ** extra - 2)).astype(jnp.int32)
    separator_rows = SR * jnp.left_shift(jnp.ones_like(level_number), level_number)
    fan_in = jnp.where(offset < 0, LM, separator_rows).astype(jnp.float32)
    row_scale = 1.0 / jnp.sqrt(fan_in * (LEVELS + 1.0))
    values = jax.random.normal(key, (total_rows, NDOF), jnp.float32)
    return (values * row_scale[:, None]).astype(jnp.bfloat16)


def levels(key, shape, cuts, least, largest):
    factor_of, own = 1.0, jax.random.fold_in(key, 6)
    for dim, shards_of in cuts:
        draws = jnp.exp(jax.random.uniform(jax.random.fold_in(own, dim), (shards_of,), jnp.float32, least / len(cuts), largest / len(cuts)))
        factor_of = factor_of * jnp.repeat(draws, shape[dim] // shards_of).reshape([-1 if axis == dim else 1 for axis in range(len(shape))])
    return factor_of


def bell_draw(stream_key, extent, deviation, most, split=(), kind=jnp.bfloat16):
    entries = deviation * jax.random.normal(stream_key, extent, jnp.float32)
    if split:
        entries = entries * levels(stream_key, extent, split, -0.22, 0.18)
    return jnp.clip(entries, -most, most).astype(kind)


def setup_inputs(seed: int = 0) -> dict:
    key_of = jax.random.split(jax.random.key(seed), 5)
    ritz_coefficients = bell_draw(key_of[0], (K, NEV), 1.0, 6.0, ((0, 8), (1, 16)))
    mode_map = jax.vmap(lambda own: jax.random.permutation(own, KM))(jax.random.split(key_of[1], NSUBS)).reshape((NSUBS, KM)).astype(jnp.int32)
    leaf_count = draw_leaf_count(jax.random.fold_in(key_of[4], 71), 0)
    mode_blocks = draw_mode_blocks(jax.random.fold_in(key_of[4], 71), 0)
    return dict(ritz_coefficients=ritz_coefficients, mode_map=mode_map, leaf_count=leaf_count, mode_blocks=mode_blocks)


def reference(ritz_coefficients, mode_map, leaf_count, mode_blocks):
    lanczos_rows = ritz_coefficients.reshape(NSUBS, KM, NEV)

    def place_rows(pair):
        source_rows, slot_order = pair
        return jnp.zeros((KM, NEV), jnp.bfloat16).at[slot_order].set(source_rows)

    coeffs = lax.map(place_rows, (lanczos_rows, mode_map))
    kept_rows = jnp.arange(LM, dtype=jnp.int32)[None, :] < leaf_count[:, None]
    leaf_rows = jnp.where(kept_rows[:, :, None], coeffs[:, :LM], jnp.zeros((), jnp.bfloat16))
    grouped = []
    for level_number in range(1, LEVELS + 1):
        own_share = coeffs[:, LM + (level_number - 1) * SR: LM + level_number * SR]
        grouped.append(own_share.reshape(NSUBS >> level_number, (2 ** level_number) * SR, NEV))
    blocks = mode_blocks.reshape(NSUBS, MCOLS, NDOF)

    def recover(triple):
        modes_block, own_leaf, device = triple
        pieces = [own_leaf]
        for level_number in range(1, LEVELS + 1):
            pieces.append(lax.dynamic_index_in_dim(grouped[level_number - 1], device >> level_number, 0, keepdims=False))
        all_coeffs = jnp.concatenate(pieces, axis=0)
        product = lax.dot_general(modes_block, all_coeffs, (((0,), (0,)), ((), ())), preferred_element_type=jnp.float32)
        return product.astype(jnp.bfloat16)

    result = lax.map(recover, (blocks, leaf_rows, jnp.arange(NSUBS, dtype=jnp.int32)))
    return result.reshape(NSUBS * NDOF, NEV)
```

```python
import functools

import jax
import jax.numpy as jnp
from jax import lax
from jax.experimental import pallas as pl
from jax.experimental.pallas import tpu as pltpu
from jax.sharding import PartitionSpec as P

SR = 16
LEVELS = 5
AXES = ("row", "sub")


OWN = [(0, l) for l in (1, 2, 3, 4, 5)]
FIRST = (
    [(2, l) for l in (2, 3, 4, 5)]
    + [(6, l) for l in (3, 4, 5)]
    + [(4, l) for l in (3, 4, 5)]
    + [(8, l) for l in (4, 5)]
    + [(16, 5)]
)
SECOND_Z = [(8 ^ m, l) for m in (2, 6, 4) for l in (4, 5)]
SECOND_X = [(16 ^ m, 5) for m in (2, 6, 4, 8)]
SECOND_XZ = [(24 ^ m, 5) for m in (2, 6, 4)]


def partner(shares):
    return [(m ^ 1, l) for m, l in shares]


CHUNKS = (
    [None, None, None] + OWN + FIRST + partner(OWN) + partner(FIRST),
    SECOND_Z + partner(SECOND_Z),
    SECOND_X + SECOND_XZ + partner(SECOND_X) + partner(SECOND_XZ),
)


def exchange(value, mask):
    return lax.ppermute(value, AXES, [(i, i ^ mask) for i in range(128)])


def arrange_kernel(blocks, *refs):
    outs, rows, sem = refs[:-2], refs[-2], refs[-1]
    device = lax.axis_index("row") * lax.axis_size("sub") + lax.axis_index("sub")
    order = [share for chunk in CHUNKS for share in chunk]
    copies = []
    for slot, share in enumerate(order):
        if share is None:
            block = slot
        else:
            mask, level = share
            block = (1 << level) + 1 + ((device ^ mask) & ((1 << level) - 1))
        copies.append(
            pltpu.make_async_copy(
                blocks.at[pl.ds(pl.multiple_of(block * SR, SR), SR), :],
                rows.at[slot * SR : (slot + 1) * SR, :],
                sem,
            )
        )
    for copy in copies:
        copy.start()
    for copy in copies:
        copy.wait()
    at = 0
    for out in outs:
        depth = out.shape[1]
        out[...] = rows[at : at + depth, :].T
        at += depth


def arrange(blocks):
    ndof = blocks.shape[1]
    return pl.pallas_call(
        arrange_kernel,
        out_shape=[jax.ShapeDtypeStruct((ndof, SR * len(c)), jnp.bfloat16) for c in CHUNKS],
        in_specs=[pl.BlockSpec(memory_space=pl.ANY)],
        out_specs=[pl.BlockSpec(memory_space=pltpu.VMEM)] * len(CHUNKS),
        scratch_shapes=[pltpu.VMEM(blocks.shape, jnp.bfloat16), pltpu.SemaphoreType.DMA],
        cost_estimate=pl.CostEstimate(flops=0, bytes_accessed=9 << 20, transcendentals=0),
        name="arrange",
    )(blocks)


TILE = 512
GRANT = 16 << 20


def product_kernel(first, last, count, modes, *refs):
    pieces, refs = refs[:count], refs[count:]
    if not first:
        total_in, refs = refs[0], refs[1:]
    if not last:
        total = refs[0]
    else:
        out, buf, sem = refs
    width = pieces[0].shape[1]
    steps = width // TILE

    def send(step):
        return pltpu.make_async_copy(
            buf.at[step % 2],
            out.at[:, pl.ds(pl.multiple_of(step * TILE, TILE), TILE)],
            sem.at[step % 2],
        )

    @pl.loop(0, steps)
    def _(step):
        columns = pl.ds(pl.multiple_of(step * TILE, TILE), TILE)
        value = jnp.dot(
            modes[...],
            jnp.concatenate([p[:, columns] for p in pieces], axis=0),
            preferred_element_type=jnp.float32,
        )
        if not first:
            value = value + total_in[:, columns]
        if not last:
            total[:, columns] = value
        else:

            @pl.when(step >= 2)
            def _():
                send(step - 2).wait()

            buf[step % 2] = value.astype(jnp.bfloat16)
            send(step).start()

    if last:
        send(steps - 2).wait()
        send(steps - 1).wait()


def product(modes, pieces, total=None, last=False, name=None):
    ndof, depth = modes.shape
    width = pieces[0].shape[1]
    first = total is None
    vmem = pl.BlockSpec(memory_space=pltpu.VMEM)
    operands = [modes, *pieces] + ([] if first else [total])
    if last:
        out_shape = jax.ShapeDtypeStruct((ndof, width), jnp.bfloat16)
        out_spec = pl.BlockSpec(memory_space=pl.ANY)
        scratch = [pltpu.VMEM((2, ndof, TILE), jnp.bfloat16), pltpu.SemaphoreType.DMA((2,))]
        alias = {}
    else:
        out_shape = pltpu.VMEM((ndof, width), jnp.float32)
        out_spec = vmem
        scratch = []
        alias = {} if first else {len(operands) - 1: 0}
    return pl.pallas_call(
        functools.partial(product_kernel, first, last, len(pieces)),
        out_shape=out_shape,
        in_specs=[vmem] * len(operands),
        out_specs=out_spec,
        scratch_shapes=scratch,
        input_output_aliases=alias,
        compiler_params=pltpu.CompilerParams(vmem_limit_bytes=GRANT),
        cost_estimate=pl.CostEstimate(
            flops=2 * ndof * width * depth, bytes_accessed=8 << 20, transcendentals=0
        ),
        name=name,
    )(*operands)


def shards(ritz_coefficients, mode_map, leaf_count, mode_blocks):
    modes = arrange(mode_blocks)
    lanczos_rows = lax.all_to_all(ritz_coefficients, "sub", split_axis=0, concat_axis=1, tiled=True)
    kept = lanczos_rows.shape[0]
    leaf = kept - LEVELS * SR
    slot_ids = lax.broadcasted_iota(jnp.int32, (kept, kept), 1)
    placement = (mode_map[0][:, None] == slot_ids).astype(jnp.bfloat16)
    coeffs = lax.dot_general(
        placement, lanczos_rows, (((0,), (0,)), ((), ())), preferred_element_type=jnp.float32
    ).astype(jnp.bfloat16)
    kept_rows = lax.broadcasted_iota(jnp.int32, (leaf, 1), 0) < leaf_count[0]
    leaf_rows = jnp.where(kept_rows, coeffs[:leaf], jnp.zeros((), jnp.bfloat16))

    def shares(low):
        return coeffs[leaf + (low - 1) * SR :]

    own = shares(1)
    f = exchange(shares(2), 2)
    g = exchange(shares(3), 6)
    h = exchange(shares(3), 4)
    z = exchange(shares(4), 8)
    x = exchange(shares(5), 16)
    own_swap = exchange(own, 1)
    z2 = exchange(jnp.concatenate([f[32:], g[16:], h[16:]]), 8)
    x2 = exchange(jnp.concatenate([f[48:], g[32:], h[32:], z[16:]]), 16)
    xz2 = exchange(jnp.concatenate([f[48:], g[32:], h[32:]]), 24)
    first_swap = exchange(jnp.concatenate([f, g, h, z, x]), 1)
    total = product(modes[0], [leaf_rows, own, f, g, h, z, x, own_swap, first_swap], name="chunk0")
    z2_swap = exchange(z2, 1)
    total = product(modes[1], [z2, z2_swap], total, name="chunk1")
    x2_swap = exchange(jnp.concatenate([x2, xz2]), 1)
    return product(modes[2], [x2, xz2, x2_swap], total, last=True, name="chunk2")


def solution(mesh):
    return jax.shard_map(
        shards,
        mesh=mesh,
        in_specs=(
            P("row", "sub"),
            P(("row", "sub"), None),
            P(("row", "sub")),
            P(("row", "sub"), None),
        ),
        out_specs=P(("row", "sub"), None),
        check_vma=False,
    )
```

```python
import functools

import jax
import jax.numpy as jnp
from jax import lax
from jax.experimental import pallas as pl
from jax.experimental.pallas import tpu as pltpu
from jax.sharding import PartitionSpec as P


SR = 16
LEVELS = 5
AXES = ("row", "sub")


OWN = [(0, l) for l in (1, 2, 3, 4, 5)]
FIRST = (
    [(2, l) for l in (2, 3, 4, 5)]
    + [(6, l) for l in (3, 4, 5)]
    + [(4, l) for l in (3, 4, 5)]
    + [(8, l) for l in (4, 5)]
    + [(16, 5), (24, 5)]
)
SECOND = (
    [(10, 4), (10, 5), (26, 5)]
    + [(14, 4), (14, 5), (30, 5)]
    + [(12, 4), (12, 5)]
    + [(18, 5), (22, 5), (20, 5)]
    + [(28, 5)]
)


def partner(shares):
    return [(m ^ 1, l) for m, l in shares]


CHUNKS = (
    [None, None, None] + OWN + partner(OWN),
    FIRST + partner(FIRST),
    SECOND + partner(SECOND),
)


def exchange(value, mask):
    return lax.ppermute(value, AXES, [(i, i ^ mask) for i in range(128)])


def arrange_kernel(blocks, *refs):
    outs, rows, sem = refs[:-2], refs[-2], refs[-1]
    device = lax.axis_index("row") * lax.axis_size("sub") + lax.axis_index("sub")
    order = [share for chunk in CHUNKS for share in chunk]
    copies = []
    for slot, share in enumerate(order):
        if share is None:
            block = slot
        else:
            mask, level = share
            block = (1 << level) + 1 + ((device ^ mask) & ((1 << level) - 1))
        copies.append(
            pltpu.make_async_copy(
                blocks.at[pl.ds(pl.multiple_of(block * SR, SR), SR), :],
                rows.at[slot * SR : (slot + 1) * SR, :],
                sem,
            )
        )
    for copy in copies:
        copy.start()
    for copy in copies:
        copy.wait()
    at = 0
    for out in outs:
        depth = out.shape[1]
        out[...] = rows[at : at + depth, :].T
        at += depth


def arrange(blocks):
    ndof = blocks.shape[1]
    return pl.pallas_call(
        arrange_kernel,
        out_shape=[pltpu.VMEM((ndof, SR * len(c)), jnp.bfloat16) for c in CHUNKS],
        in_specs=[pl.BlockSpec(memory_space=pl.ANY)],
        out_specs=[pl.BlockSpec(memory_space=pltpu.VMEM)] * len(CHUNKS),
        scratch_shapes=[pltpu.VMEM(blocks.shape, jnp.bfloat16), pltpu.SemaphoreType.DMA],
        compiler_params=pltpu.CompilerParams(vmem_limit_bytes=GRANT),
        cost_estimate=pl.CostEstimate(flops=0, bytes_accessed=9 << 20, transcendentals=0),
        name="arrange",
    )(blocks)


TILE = 512
GRANT = 12 << 20
SMALL = 4 << 20


def product_kernel(first, last, count, modes, *refs):
    pieces, refs = refs[:count], refs[count:]
    if not first:
        total_in, refs = refs[0], refs[1:]
    if not last:
        total = refs[0]
    else:
        out, buf, sem = refs
    width = pieces[0].shape[1]
    steps = width // TILE

    def send(step):
        return pltpu.make_async_copy(
            buf.at[step % 2],
            out.at[:, pl.ds(pl.multiple_of(step * TILE, TILE), TILE)],
            sem.at[step % 2],
        )

    @pl.loop(0, steps)
    def _(step):
        columns = pl.ds(pl.multiple_of(step * TILE, TILE), TILE)
        value = jnp.dot(
            modes[...],
            jnp.concatenate([p[:, columns] for p in pieces], axis=0),
            preferred_element_type=jnp.float32,
        )
        if not first:
            value = value + total_in[:, columns]
        if not last:
            total[:, columns] = value
        else:

            @pl.when(step >= 2)
            def _():
                send(step - 2).wait()

            buf[step % 2] = value.astype(jnp.bfloat16)
            send(step).start()

    if last:
        send(steps - 2).wait()
        send(steps - 1).wait()


def product(modes, pieces, total=None, last=False):
    ndof, depth = modes.shape
    width = pieces[0].shape[1]
    first = total is None
    vmem = pl.BlockSpec(memory_space=pltpu.VMEM)
    operands = [modes, *pieces] + ([] if first else [total])
    if last:
        out_shape = jax.ShapeDtypeStruct((ndof, width), jnp.bfloat16)
        out_spec = pl.BlockSpec(memory_space=pl.ANY)
        scratch = [pltpu.VMEM((2, ndof, TILE), jnp.bfloat16), pltpu.SemaphoreType.DMA((2,))]
        alias = {}
    else:
        out_shape = pltpu.VMEM((ndof, width), jnp.float32)
        out_spec = vmem
        scratch = []
        alias = {} if first else {len(operands) - 1: 0}
    return pl.pallas_call(
        functools.partial(product_kernel, first, last, len(pieces)),
        out_shape=out_shape,
        in_specs=[vmem] * len(operands),
        out_specs=out_spec,
        scratch_shapes=scratch,
        input_output_aliases=alias,
        compiler_params=pltpu.CompilerParams(vmem_limit_bytes=GRANT),
        cost_estimate=pl.CostEstimate(
            flops=2 * ndof * width * depth, bytes_accessed=8 << 20, transcendentals=0
        ),
    )(*operands)


def place_kernel(leaf, count, slots, blocks, _, out):
    kept = out.shape[0]
    rows = lax.broadcasted_iota(jnp.int32, (kept, kept), 0)
    live = (rows >= leaf) | (rows < count[0])
    pick = jnp.where((rows == slots[...]) & live, 1.0, 0.0).astype(jnp.bfloat16)
    for part in range(blocks.shape[0]):
        columns = slice(part * blocks.shape[2], (part + 1) * blocks.shape[2])
        out[:, columns] = jnp.dot(
            pick, blocks[part], preferred_element_type=jnp.float32
        ).astype(jnp.bfloat16)


def place(mode_map, leaf_count, blocks, after):
    parts, kept, width = blocks.shape
    return pl.pallas_call(
        functools.partial(place_kernel, kept - LEVELS * SR),
        out_shape=pltpu.VMEM((kept, parts * width), jnp.bfloat16),
        in_specs=[
            pl.BlockSpec(memory_space=pltpu.SMEM),
            pl.BlockSpec(memory_space=pltpu.VMEM),
            pl.BlockSpec(memory_space=pltpu.VMEM),
            pl.BlockSpec(memory_space=pl.ANY),
        ],
        out_specs=pl.BlockSpec(memory_space=pltpu.VMEM),
        compiler_params=pltpu.CompilerParams(vmem_limit_bytes=SMALL),
        name="place",
    )(leaf_count, mode_map, blocks, after)


def pack_kernel(starts, count, *refs):
    out, at = refs[-1], 0
    for start, piece in zip(starts, refs[:count]):
        depth = piece.shape[0] - start
        out[at : at + depth, :] = piece[start:, :]
        at += depth


def pack(pieces, starts, *after):
    depth = sum(p.shape[0] - s for p, s in zip(pieces, starts))
    return pl.pallas_call(
        functools.partial(pack_kernel, starts, len(pieces)),
        out_shape=pltpu.VMEM((depth, pieces[0].shape[1]), jnp.bfloat16),
        in_specs=[pl.BlockSpec(memory_space=pltpu.VMEM)] * len(pieces)
        + [pl.BlockSpec(memory_space=pl.ANY)] * len(after),
        out_specs=pl.BlockSpec(memory_space=pltpu.VMEM),
        compiler_params=pltpu.CompilerParams(vmem_limit_bytes=SMALL),
    )(*pieces, *after)


def shards(ritz_coefficients, mode_map, leaf_count, mode_blocks):
    modes = arrange(mode_blocks)
    parts = lax.axis_size("sub")
    width = ritz_coefficients.shape[1]
    blocks = ritz_coefficients.reshape(parts, -1, width)
    blocks = lax.all_to_all(blocks, "sub", split_axis=0, concat_axis=0, tiled=True)
    coeffs = place(mode_map, leaf_count, blocks, modes[0])
    leaf = coeffs.shape[0] - LEVELS * SR

    def shares(low):
        return coeffs[leaf + (low - 1) * SR :]

    own = shares(1)
    h = exchange(shares(3), 4)
    f = exchange(shares(2), 2)
    g = exchange(shares(3), 6)
    z = exchange(shares(4), 8)
    x = exchange(shares(5), 16)
    xz = exchange(shares(5), 24)
    total = product(modes[0], [coeffs[:leaf], own, exchange(own, 1)])
    along_y = pack([z, xz], [0, 0], total)
    along_x = pack([f, g, h], [48, 32, 32], total)
    first = [f, g, h, z, x, xz]
    second = [
        exchange(along_y, 2),
        exchange(along_y, 6),
        exchange(h[16:], 8),
        exchange(along_x, 16),
        exchange(h[32:], 24),
    ]
    first += [exchange(p, 1) for p in first]
    total = product(modes[1], first, total)
    second += [exchange(p, 1) for p in second]
    return product(modes[2], second, total, last=True)


def solution(mesh):
    return jax.shard_map(
        shards,
        mesh=mesh,
        in_specs=(
            P("row", "sub"),
            P(("row", "sub"), None),
            P(("row", "sub")),
            P(("row", "sub"), None),
        ),
        out_specs=P(("row", "sub"), None),
        check_vma=False,
    )
```

```python
import functools

import jax
import jax.numpy as jnp
from jax import lax
from jax.experimental import pallas as pl
from jax.experimental.pallas import tpu as pltpu
from jax.sharding import PartitionSpec as P


SR = 16
LEVELS = 5
AXES = ("row", "sub")


OWN = [(0, l) for l in (1, 2, 3, 4, 5)]
FIRST = (
    [(2, l) for l in (2, 3, 4, 5)]
    + [(6, l) for l in (3, 4, 5)]
    + [(4, l) for l in (3, 4, 5)]
    + [(8, l) for l in (4, 5)]
    + [(16, 5), (24, 5)]
)
SECOND = (
    [(10, 4), (10, 5), (26, 5)]
    + [(14, 4), (14, 5), (30, 5)]
    + [(12, 4), (12, 5)]
    + [(18, 5), (22, 5), (20, 5)]
    + [(28, 5)]
)


def partner(shares):
    return [(m ^ 1, l) for m, l in shares]


CHUNKS = (
    [None, None, None] + OWN + partner(OWN),
    FIRST + partner(FIRST),
    SECOND + partner(SECOND),
)


def exchange(value, mask):
    return lax.ppermute(value, AXES, [(i, i ^ mask) for i in range(128)])


def arrange_kernel(leaf, count, slots, blocks, *refs):
    outs, pick, rows, sem = refs[:-3], refs[-3], refs[-2], refs[-1]
    device = lax.axis_index("row") * lax.axis_size("sub") + lax.axis_index("sub")
    slot, waits = 0, []
    for number, chunk in enumerate(CHUNKS):
        copies = []
        for share in chunk:
            if share is None:
                block = slot
            else:
                mask, level = share
                block = (1 << level) + 1 + ((device ^ mask) & ((1 << level) - 1))
            copies.append(
                pltpu.make_async_copy(
                    blocks.at[pl.ds(pl.multiple_of(block * SR, SR), SR), :],
                    rows.at[slot * SR : (slot + 1) * SR, :],
                    sem.at[number],
                )
            )
            slot += 1
        for copy in copies:
            copy.start()
        waits.append(copies)
    local = lax.broadcasted_iota(jnp.int32, pick.shape, 0)
    live = (local >= leaf) | (local < count[0])
    pick[...] = jnp.where((local == slots[...]) & live, 1.0, 0.0).astype(jnp.bfloat16)
    at = 0
    for number, copies in enumerate(waits):
        for copy in copies:
            copy.wait()
        depth = SR * len(copies)
        outs[number][...] = rows[at : at + depth, :].T
        at += depth


def arrange(leaf_count, mode_map, blocks):
    ndof = blocks.shape[1]
    kept = mode_map.shape[1]
    vmem = pl.BlockSpec(memory_space=pltpu.VMEM)
    return pl.pallas_call(
        functools.partial(arrange_kernel, kept - LEVELS * SR),
        out_shape=[pltpu.VMEM((ndof, SR * len(c)), jnp.bfloat16) for c in CHUNKS]
        + [pltpu.VMEM((kept, kept), jnp.bfloat16)],
        in_specs=[
            pl.BlockSpec(memory_space=pltpu.SMEM),
            vmem,
            pl.BlockSpec(memory_space=pltpu.HBM),
        ],
        out_specs=[vmem] * (len(CHUNKS) + 1),
        scratch_shapes=[
            pltpu.VMEM(blocks.shape, jnp.bfloat16),
            pltpu.SemaphoreType.DMA((len(CHUNKS),)),
        ],
        compiler_params=pltpu.CompilerParams(vmem_limit_bytes=GRANT),
        cost_estimate=pl.CostEstimate(flops=0, bytes_accessed=9 << 20, transcendentals=0),
        name="arrange",
    )(leaf_count, mode_map, pltpu.with_memory_space_constraint(blocks, pltpu.HBM))


GRANT = 20 << 20
SMALL = 4 << 20


def product_kernel(first, last, tiles, count, modes, *refs):
    pieces, refs = refs[:count], refs[count:]
    if not first:
        total_in, refs = refs[0], refs[1:]
    if last:
        out, buf, sem = refs
    else:
        total = refs[0]
    sends = []
    for number, (at, height) in enumerate(tiles):
        rows = slice(at, at + height)
        value = jnp.dot(
            modes[rows, :],
            jnp.concatenate([p[...] for p in pieces], axis=0),
            preferred_element_type=jnp.float32,
        )
        if not first:
            value = value + total_in[rows, :]
        if last:
            buf[rows, :] = value.astype(jnp.bfloat16)
            sends.append(pltpu.make_async_copy(buf.at[rows, :], out.at[rows, :], sem.at[number]))
            sends[-1].start()
        else:
            total[rows, :] = value
    for send in sends:
        send.wait()


def product(number, modes, pieces, total=None, last=False):
    ndof = modes[number].shape[0]
    depth = SR * len(CHUNKS[number])
    width = pieces[0].shape[1]
    first = total is None
    vmem = pl.BlockSpec(memory_space=pltpu.VMEM)
    operands = [modes[number], *pieces] + ([] if first else [total])
    heights = LAST_TILES if last else TILES
    tiles, at = [], 0
    for height in heights:
        tiles.append((at, height))
        at += height
    if last:
        out_shape = jax.ShapeDtypeStruct((ndof, width), jnp.bfloat16)
        out_spec = pl.BlockSpec(memory_space=pl.ANY)
        scratch = [pltpu.VMEM((ndof, width), jnp.bfloat16), pltpu.SemaphoreType.DMA((len(tiles),))]
        alias = {}
    else:
        out_shape = pltpu.VMEM((ndof, width), jnp.float32)
        out_spec = vmem
        scratch = []
        alias = {} if first else {len(operands) - 1: 0}
    return pl.pallas_call(
        functools.partial(product_kernel, first, last, tiles, len(pieces)),
        out_shape=out_shape,
        in_specs=[vmem] * len(operands),
        out_specs=out_spec,
        scratch_shapes=scratch,
        input_output_aliases=alias,
        compiler_params=pltpu.CompilerParams(vmem_limit_bytes=GRANT),
        cost_estimate=pl.CostEstimate(
            flops=2 * ndof * width * depth, bytes_accessed=8 << 20, transcendentals=0
        ),
    )(*operands)


TILES = (1024, 1024)
LAST_TILES = (1024, 768, 256)


def place_kernel(pick, blocks, _, out):
    for part in range(blocks.shape[0]):
        columns = slice(part * blocks.shape[2], (part + 1) * blocks.shape[2])
        out[:, columns] = jnp.dot(
            pick[...], blocks[part], preferred_element_type=jnp.float32
        ).astype(jnp.bfloat16)


def place(pick, blocks, after):
    parts, kept, width = blocks.shape
    vmem = pl.BlockSpec(memory_space=pltpu.VMEM)
    return pl.pallas_call(
        place_kernel,
        out_shape=pltpu.VMEM((kept, parts * width), jnp.bfloat16),
        in_specs=[vmem, vmem, pl.BlockSpec(memory_space=pl.ANY)],
        out_specs=vmem,
        compiler_params=pltpu.CompilerParams(vmem_limit_bytes=SMALL),
        name="place",
    )(pick, blocks, after)


def pack_kernel(starts, *refs):
    out, at = refs[-1], 0
    for start, piece in zip(starts, refs):
        depth = piece.shape[0] - start
        out[at : at + depth, :] = piece[start:, :]
        at += depth


def pack(pieces, starts):
    depth = sum(p.shape[0] - s for p, s in zip(pieces, starts))
    return pl.pallas_call(
        functools.partial(pack_kernel, starts),
        out_shape=pltpu.VMEM((depth, pieces[0].shape[1]), jnp.bfloat16),
        in_specs=[pl.BlockSpec(memory_space=pltpu.VMEM)] * len(pieces),
        out_specs=pl.BlockSpec(memory_space=pltpu.VMEM),
        compiler_params=pltpu.CompilerParams(vmem_limit_bytes=SMALL),
    )(*pieces)


def shards(ritz_coefficients, mode_map, leaf_count, mode_blocks):
    *modes, pick = arrange(leaf_count, mode_map, mode_blocks)
    parts = lax.axis_size("sub")
    width = ritz_coefficients.shape[1]
    blocks = ritz_coefficients.reshape(parts, -1, width)
    blocks = lax.all_to_all(blocks, "sub", split_axis=0, concat_axis=0, tiled=True)
    coeffs = place(pick, blocks, modes[0])
    leaf = coeffs.shape[0] - LEVELS * SR

    def shares(low):
        return coeffs[leaf + (low - 1) * SR :]

    own = shares(1)
    h = exchange(shares(3), 4)
    f = exchange(shares(2), 2)
    g = exchange(shares(3), 6)
    z = exchange(shares(4), 8)
    x = exchange(shares(5), 16)
    xz = exchange(shares(5), 24)
    total = product(0, modes, [coeffs[:leaf], own, exchange(own, 1)])
    along_y = pack([z, xz], [0, 0])
    along_x = pack([f, g, h], [48, 32, 32])
    first = [f, g, h, z, x, xz]
    second = [
        exchange(along_y, 2),
        exchange(along_y, 6),
        exchange(h[16:], 8),
        exchange(along_x, 16),
        exchange(h[32:], 24),
    ]
    first += [exchange(p, 1) for p in first]
    total = product(1, modes, first, total)
    second += [exchange(p, 1) for p in second]
    return product(2, modes, second, total, last=True)


def solution(mesh):
    return jax.shard_map(
        shards,
        mesh=mesh,
        in_specs=(
            P("row", "sub"),
            P(("row", "sub"), None),
            P(("row", "sub")),
            P(("row", "sub"), None),
        ),
        out_specs=P(("row", "sub"), None),
        check_vma=False,
    )
```

```python
import functools

import jax
import jax.numpy as jnp
from jax import lax
from jax.experimental import pallas as pl
from jax.experimental.pallas import tpu as pltpu
from jax.sharding import PartitionSpec as P


SR = 16
LEVELS = 5
LEAF = 48
PAIR = 2 * SR
AXES = ("row", "sub")


OWN = [(0, l) for l in (1, 2, 3, 4, 5)]
FIRST = (
    [(2, l) for l in (2, 3, 4, 5)]
    + [(6, l) for l in (3, 4, 5)]
    + [(4, l) for l in (3, 4, 5)]
    + [(16, 5)]
    + [(8, l) for l in (4, 5)]
    + [(24, 5)]
)
SECOND = (
    [(10, 4), (10, 5), (26, 5)]
    + [(14, 4), (14, 5), (30, 5)]
    + [(12, 4), (12, 5)]
    + [(18, 5), (22, 5), (20, 5)]
    + [(28, 5)]
)
CHUNKS = ([None] + OWN, FIRST, SECOND)
DEPTHS = (LEAF + PAIR * len(OWN), PAIR * len(FIRST), PAIR * len(SECOND))

GRANT = 20 << 20
SMALL = 6 << 20
TILES = (2048,)
LAST_TILES = (1024, 768, 256)

VMEM = pl.BlockSpec(memory_space=pltpu.VMEM)
ANY = pl.BlockSpec(memory_space=pl.ANY)


def exchange(value, mask):
    return lax.ppermute(value, AXES, [(i, i ^ mask) for i in range(128)])


def params(limit):
    return pltpu.CompilerParams(vmem_limit_bytes=limit)


def arrange_kernel(count, mine, theirs, blocks, *refs):
    outs, pick, rows, sem = refs[:-3], refs[-3], refs[-2], refs[-1]
    device = lax.axis_index("row") * lax.axis_size("sub") + lax.axis_index("sub")
    at, waits = 0, []
    for number, chunk in enumerate(CHUNKS):
        copies = []
        for share in chunk:
            if share is None:
                depth, start = LEAF, 0
            else:
                mask, level = share
                depth = PAIR
                peer = ((device ^ mask) & ((1 << level) - 1)) >> 1
                start = pl.multiple_of(SR * ((1 << level) + 1) + peer * PAIR, SR)
            copies.append(
                pltpu.make_async_copy(
                    blocks.at[pl.ds(start, depth), :], rows.at[at : at + depth, :], sem.at[number]
                )
            )
            at += depth
        for copy in copies:
            copy.start()
        waits.append(copies)
    upper = lax.axis_index("sub") % 2 == 1
    local = lax.broadcasted_iota(jnp.int32, pick.shape[1:], 0)
    for core in range(2):
        slots = jnp.where(upper == (core == 1), mine[...], theirs[...])
        pick[core] = jnp.where(local == slots, 1.0, 0.0).astype(jnp.bfloat16)
    at = 0
    for number, copies in enumerate(waits):
        for copy in copies:
            copy.wait()
        depth = DEPTHS[number]
        value = rows[at : at + depth, :]
        if number == 0:
            row = lax.broadcasted_iota(jnp.int32, (LEAF, value.shape[1]), 0)
            leaf = jnp.where(row < count[0], value[:LEAF].astype(jnp.float32), 0.0)
            value = jnp.concatenate([leaf.astype(jnp.bfloat16), value[LEAF:]], axis=0)
        outs[number][...] = value.T
        at += depth


def arrange(leaf_count, mine, theirs, blocks):
    ndof = blocks.shape[1]
    kept = mine.shape[1]
    return pl.pallas_call(
        arrange_kernel,
        out_shape=[pltpu.VMEM((ndof, depth), jnp.bfloat16) for depth in DEPTHS]
        + [pltpu.VMEM((2, kept, kept), jnp.bfloat16)],
        in_specs=[
            pl.BlockSpec(memory_space=pltpu.SMEM),
            VMEM,
            VMEM,
            pl.BlockSpec(memory_space=pltpu.HBM),
        ],
        out_specs=[VMEM] * (len(DEPTHS) + 1),
        scratch_shapes=[
            pltpu.VMEM(blocks.shape, jnp.bfloat16),
            pltpu.SemaphoreType.DMA((len(DEPTHS),)),
        ],
        compiler_params=params(GRANT),
        cost_estimate=pl.CostEstimate(flops=0, bytes_accessed=9 << 20, transcendentals=0),
        name="arrange",
    )(leaf_count, mine, theirs, pltpu.with_memory_space_constraint(blocks, pltpu.HBM))


def place_kernel(pick, blocks, _, own, swap):
    upper = lax.axis_index("sub") % 2 == 1
    width = blocks.shape[2]
    kept = pick.shape[1]
    for part in range(blocks.shape[0]):
        columns = slice(part * width, (part + 1) * width)
        even, odd = (
            jnp.dot(
                pick[core],
                blocks[part, core * kept : (core + 1) * kept, :],
                preferred_element_type=jnp.float32,
            )
            for core in range(2)
        )
        own[:LEAF, columns] = jnp.where(upper, odd[:LEAF], even[:LEAF]).astype(jnp.bfloat16)
        swap[:LEAF, columns] = jnp.where(upper, even[:LEAF], odd[:LEAF]).astype(jnp.bfloat16)
        for level in range(LEVELS):
            source = slice(LEAF + level * SR, LEAF + (level + 1) * SR)
            target = LEAF + level * PAIR
            for value in (even, odd):
                share = value[source].astype(jnp.bfloat16)
                own[target : target + SR, columns] = share
                swap[target : target + SR, columns] = share
                target += SR


def place(pick, blocks, after):
    parts, _, width = blocks.shape
    shape = pltpu.VMEM((DEPTHS[0], parts * width), jnp.bfloat16)
    return pl.pallas_call(
        place_kernel,
        out_shape=[shape, shape],
        in_specs=[VMEM, VMEM, ANY],
        out_specs=[VMEM, VMEM],
        compiler_params=params(SMALL),
        name="place",
    )(pick, blocks, after)


def collect_kernel(parts, *refs):
    count = len(refs) - len(parts)
    for part, out in zip(parts, refs[count:]):
        at = 0
        for index, start in part:
            depth = refs[index].shape[0] - start
            out[at : at + depth, :] = refs[index][start:, :]
            at += depth


def collect(pieces, parts):
    width = pieces[0].shape[1]
    return pl.pallas_call(
        functools.partial(collect_kernel, parts),
        out_shape=[
            pltpu.VMEM((sum(pieces[i].shape[0] - s for i, s in part), width), jnp.bfloat16)
            for part in parts
        ],
        in_specs=[VMEM] * len(pieces),
        out_specs=[VMEM] * len(parts),
        compiler_params=params(SMALL),
    )(*pieces)


def spans(heights):
    at = 0
    for height in heights:
        yield slice(at, at + height)
        at += height


def product_kernel(first, modes, own, got, *refs):
    total = refs[-1]
    width = own.shape[1]
    for lane, piece in enumerate((own, got)):
        columns = slice(lane * width, (lane + 1) * width)
        for rows in spans(TILES):
            value = jnp.dot(modes[rows, :], piece[...], preferred_element_type=jnp.float32)
            if not first:
                value = value + refs[0][rows, columns]
            total[rows, columns] = value


def product(modes, own, got, total=None):
    ndof, depth = modes.shape
    width = 2 * own.shape[1]
    operands = [modes, own, got] + ([] if total is None else [total])
    return pl.pallas_call(
        functools.partial(product_kernel, total is None),
        out_shape=pltpu.VMEM((ndof, width), jnp.float32),
        in_specs=[VMEM] * len(operands),
        out_specs=VMEM,
        input_output_aliases={} if total is None else {3: 0},
        compiler_params=params(GRANT),
        cost_estimate=pl.CostEstimate(
            flops=2 * ndof * width * depth, bytes_accessed=8 << 20, transcendentals=0
        ),
    )(*operands)


def finish_kernel(lane, modes, piece, total, *refs):
    out, buf, sem = refs[-3:]
    width = piece.shape[1]
    columns = slice(lane * width, (lane + 1) * width)
    core = lax.axis_index("sub") % 2
    core = 1 - core if lane else core
    sends = []
    for number, rows in enumerate(spans(LAST_TILES)):
        value = jnp.dot(modes[rows, :], piece[...], preferred_element_type=jnp.float32)
        buf[rows, :] = (value + total[rows, columns]).astype(jnp.bfloat16)
        for part in range(width // 128):
            target = pl.multiple_of((2 * part + core) * 128, 128)
            sends.append(
                pltpu.make_async_copy(
                    buf.at[rows, part * 128 : (part + 1) * 128],
                    out.at[rows, pl.ds(target, 128)],
                    sem.at[number],
                )
            )
            sends[-1].start()
    for send in sends:
        send.wait()


def finish(lane, modes, piece, total, out=None):
    ndof, depth = modes.shape
    width = piece.shape[1]
    operands = [modes, piece, total] + ([] if out is None else [out])
    return pl.pallas_call(
        functools.partial(finish_kernel, lane),
        out_shape=jax.ShapeDtypeStruct((ndof, 2 * width), jnp.bfloat16),
        in_specs=[VMEM] * 3 + [ANY] * (len(operands) - 3),
        out_specs=ANY,
        scratch_shapes=[
            pltpu.VMEM((ndof, width), jnp.bfloat16),
            pltpu.SemaphoreType.DMA((len(LAST_TILES),)),
        ],
        input_output_aliases={} if out is None else {3: 0},
        compiler_params=params(GRANT),
        cost_estimate=pl.CostEstimate(
            flops=2 * ndof * width * depth, bytes_accessed=8 << 20, transcendentals=0
        ),
    )(*operands)


def shards(ritz_coefficients, mode_map, leaf_count, mode_blocks):
    *modes, pick = arrange(leaf_count, mode_map, exchange(mode_map, 1), mode_blocks)
    parts = lax.axis_size("sub") // 2
    width = ritz_coefficients.shape[1]
    lanes = [[2 * part + core for part in range(parts)] for core in range(2)]
    blocks = lax.all_to_all(
        ritz_coefficients.reshape(parts, -1, width),
        "sub",
        split_axis=0,
        concat_axis=0,
        tiled=True,
        axis_index_groups=lanes,
    )
    own, swap = place(pick, blocks, modes[0])

    def shares(low):
        return own[LEAF + (low - 1) * PAIR :]

    got = exchange(swap, 1)
    f = exchange(shares(2), 2)
    g = exchange(shares(3), 6)
    h = exchange(shares(3), 4)
    z = exchange(shares(4), 8)
    x = exchange(shares(5), 16)
    xz = exchange(shares(5), 24)
    total = product(modes[0], own, got)
    own, along_y, along_x = collect(
        [f, g, h, x, z, xz],
        [
            [(i, 0) for i in range(6)],
            [(4, 0), (5, 0)],
            [(0, 3 * PAIR), (1, 2 * PAIR), (2, 2 * PAIR)],
        ],
    )
    second = [
        exchange(along_y, 2),
        exchange(along_y, 6),
        exchange(h[PAIR:], 8),
        exchange(along_x, 16),
        exchange(h[2 * PAIR :], 24),
    ]
    got = exchange(own, 1)
    total = product(modes[1], own, got, total)
    (own,) = collect(second, [[(i, 0) for i in range(5)]])
    got = exchange(own, 1)
    out = finish(0, modes[2], own, total)
    return finish(1, modes[2], got, total, out)


def solution(mesh):
    return jax.shard_map(
        shards,
        mesh=mesh,
        in_specs=(
            P("row", "sub"),
            P(("row", "sub"), None),
            P(("row", "sub")),
            P(("row", "sub"), None),
        ),
        out_specs=P(("row", "sub"), None),
        check_vma=False,
    )
```

```python
import functools

import jax
import jax.numpy as jnp
from jax import lax
from jax.experimental import pallas as pl
from jax.experimental.pallas import tpu as pltpu
from jax.sharding import PartitionSpec as P


SR = 16
LEAF = 48
PAIR = 2 * SR
AXES = ("row", "sub")


LAID = (1, 2, 4, 5, 3)
OWN = [(0, l) for l in LAID]
FIRST = (
    [(m, l) for m in (2, 6) for l in (5, 3)]
    + [(4, l) for l in (4, 5)]
    + [(16, 5)]
    + [(8, l) for l in (4, 5)]
    + [(24, 5)]
)
SECOND = (
    [(10, 4), (10, 5), (26, 5), (2, 2), (2, 4)]
    + [(14, 4), (14, 5), (30, 5), (4, 3), (6, 4)]
    + [(12, 4), (12, 5)]
    + [(18, 5), (22, 5), (20, 5)]
    + [(28, 5)]
)
CHUNKS = ([None] + OWN, FIRST, SECOND)
DEPTHS = (LEAF + PAIR * len(OWN), PAIR * len(FIRST), PAIR * len(SECOND))

GRANT = 20 << 20
SMALL = 6 << 20
TILES = (1024, 1024)
LAST_TILES = (768, 768, 512)
EARLY = 1024

VMEM = pl.BlockSpec(memory_space=pltpu.VMEM)
HBM = pl.BlockSpec(memory_space=pltpu.HBM)
ANY = pl.BlockSpec(memory_space=pl.ANY)


def in_hbm(value):
    return pltpu.with_memory_space_constraint(value, pltpu.HBM)


def exchange(value, mask):
    return lax.ppermute(value, AXES, [(i, i ^ mask) for i in range(128)])


def params(limit):
    return pltpu.CompilerParams(vmem_limit_bytes=limit)


def arrange_kernel(count, mine_hbm, theirs, blocks, *refs):
    outs, (pick, rows, mine, sem) = refs[:-4], refs[-4:]
    own_map = pltpu.make_async_copy(mine_hbm, mine, sem.at[len(DEPTHS)])
    own_map.start()
    device = lax.axis_index("row") * lax.axis_size("sub") + lax.axis_index("sub")
    at, waits = 0, []
    for number, chunk in enumerate(CHUNKS):
        copies = []
        for share in chunk:
            if share is None:
                depth, start = LEAF, 0
            else:
                mask, level = share
                depth = PAIR
                peer = ((device ^ mask) & ((1 << level) - 1)) >> 1
                start = pl.multiple_of(SR * ((1 << level) + 1) + peer * PAIR, SR)
            copies.append(
                pltpu.make_async_copy(
                    blocks.at[pl.ds(start, depth), :], rows.at[at : at + depth, :], sem.at[number]
                )
            )
            at += depth
        for copy in copies:
            copy.start()
        waits.append(copies)
    own_map.wait()
    upper = lax.axis_index("sub") % 2 == 1
    local = lax.broadcasted_iota(jnp.int32, pick.shape[1:], 0)
    for core in range(2):
        slots = jnp.where(upper == (core == 1), mine[...], theirs[...])
        pick[core] = jnp.where(local == slots, 1.0, 0.0).astype(jnp.bfloat16)
    at = 0
    for number, copies in enumerate(waits):
        for copy in copies:
            copy.wait()
        depth = DEPTHS[number]
        value = rows[at : at + depth, :]
        if number == 0:
            row = lax.broadcasted_iota(jnp.int32, (LEAF, value.shape[1]), 0)
            leaf = jnp.where(row < count[0], value[:LEAF].astype(jnp.float32), 0.0)
            value = jnp.concatenate([leaf.astype(jnp.bfloat16), value[LEAF:]], axis=0)
        outs[number][...] = value.T
        at += depth


def arrange(leaf_count, mine, theirs, blocks):
    ndof = blocks.shape[1]
    kept = mine.shape[1]
    return pl.pallas_call(
        arrange_kernel,
        out_shape=[pltpu.VMEM((ndof, depth), jnp.bfloat16) for depth in DEPTHS]
        + [pltpu.VMEM((2, kept, kept), jnp.bfloat16)],
        in_specs=[
            pl.BlockSpec(memory_space=pltpu.SMEM),
            HBM,
            VMEM,
            HBM,
        ],
        out_specs=[VMEM] * (len(DEPTHS) + 1),
        scratch_shapes=[
            pltpu.VMEM(blocks.shape, jnp.bfloat16),
            pltpu.VMEM(mine.shape, mine.dtype),
            pltpu.SemaphoreType.DMA((len(DEPTHS) + 1,)),
        ],
        compiler_params=params(GRANT),
        cost_estimate=pl.CostEstimate(flops=0, bytes_accessed=9 << 20, transcendentals=0),
        name="arrange",
    )(leaf_count, in_hbm(mine), theirs, in_hbm(blocks))


def place_kernel(pick, blocks, _, own, swap):
    upper = lax.axis_index("sub") % 2 == 1
    width = blocks.shape[2]
    kept = pick.shape[1]
    for part in range(blocks.shape[0]):
        columns = slice(part * width, (part + 1) * width)
        even, odd = (
            jnp.dot(
                pick[core],
                blocks[part, core * kept : (core + 1) * kept, :],
                preferred_element_type=jnp.float32,
            )
            for core in range(2)
        )
        own[:LEAF, columns] = jnp.where(upper, odd[:LEAF], even[:LEAF]).astype(jnp.bfloat16)
        swap[:LEAF, columns] = jnp.where(upper, even[:LEAF], odd[:LEAF]).astype(jnp.bfloat16)
        for place, level in enumerate(LAID):
            source = slice(LEAF + (level - 1) * SR, LEAF + level * SR)
            target = LEAF + place * PAIR
            for value in (even, odd):
                share = value[source].astype(jnp.bfloat16)
                own[target : target + SR, columns] = share
                swap[target : target + SR, columns] = share
                target += SR


def place(pick, blocks, after):
    parts, _, width = blocks.shape
    shape = pltpu.VMEM((DEPTHS[0], parts * width), jnp.bfloat16)
    return pl.pallas_call(
        place_kernel,
        out_shape=[shape, shape],
        in_specs=[VMEM, VMEM, ANY],
        out_specs=[VMEM, VMEM],
        compiler_params=params(SMALL),
        name="place",
    )(pick, blocks, after)


def cut(piece, start, stop):
    return (piece.shape[0] if stop is None else stop) - start


def collect_kernel(parts, *refs):
    count = len(refs) - len(parts)
    for part, out in zip(parts, refs[count:]):
        at = 0
        for index, start, stop in part:
            depth = cut(refs[index], start, stop)
            out[at : at + depth, :] = refs[index][start : start + depth, :]
            at += depth


def collect(pieces, parts):
    width = pieces[0].shape[1]
    return pl.pallas_call(
        functools.partial(collect_kernel, parts),
        out_shape=[
            pltpu.VMEM((sum(cut(pieces[i], a, b) for i, a, b in part), width), jnp.bfloat16)
            for part in parts
        ],
        in_specs=[VMEM] * len(pieces),
        out_specs=[VMEM] * len(parts),
        compiler_params=params(SMALL),
    )(*pieces)


def spans(heights):
    at = 0
    for height in heights:
        yield slice(at, at + height)
        at += height


def product_kernel(first, modes, own, got, *refs):
    total = refs[-1]
    piece = jnp.concatenate([own[...], got[...]], axis=1)
    for rows in spans(TILES):
        value = jnp.dot(modes[rows, :], piece, preferred_element_type=jnp.float32)
        if not first:
            value = value + refs[0][rows, :]
        total[rows, :] = value


def product(modes, own, got, total=None):
    ndof, depth = modes.shape
    width = 2 * own.shape[1]
    operands = [modes, own, got] + ([] if total is None else [total])
    return pl.pallas_call(
        functools.partial(product_kernel, total is None),
        out_shape=pltpu.VMEM((ndof, width), jnp.float32),
        in_specs=[VMEM] * len(operands),
        out_specs=VMEM,
        input_output_aliases={} if total is None else {3: 0},
        compiler_params=params(GRANT),
        cost_estimate=pl.CostEstimate(
            flops=2 * ndof * width * depth, bytes_accessed=8 << 20, transcendentals=0
        ),
    )(*operands)


def lane_sends(source, at, rows, out, core, sem):
    depth = rows.stop - rows.start
    return [
        pltpu.make_async_copy(
            source.at[at : at + depth, part * 128 : (part + 1) * 128],
            out.at[rows, pl.ds(pl.multiple_of((2 * part + core) * 128, 128), 128)],
            sem,
        )
        for part in range(source.shape[1] // 128)
    ]


def own_lane_kernel(modes, piece, total, out, rest, buf, sem):
    core = lax.axis_index("sub") % 2
    width = piece.shape[1]
    early, late = spans((buf.shape[0], rest.shape[0]))
    sends = []
    for rows, target in ((early, buf), (late, rest)):
        value = jnp.dot(modes[rows, :], piece[...], preferred_element_type=jnp.float32)
        target[...] = (value + total[rows, :width]).astype(jnp.bfloat16)
        if target is buf:
            sends = lane_sends(buf, 0, rows, out, core, sem)
            for send in sends:
                send.start()
    for send in sends:
        send.wait()


def last_kernel(modes, piece, total, rest, _, out, buf, sem):
    core = lax.axis_index("sub") % 2
    width = piece.shape[1]
    late = slice(modes.shape[0] - rest.shape[0], modes.shape[0])
    started = lane_sends(rest, 0, late, out, core, sem.at[len(LAST_TILES)])
    for send in started:
        send.start()
    for number, rows in enumerate(spans(LAST_TILES)):
        value = jnp.dot(modes[rows, :], piece[...], preferred_element_type=jnp.float32)
        buf[rows, :] = (value + total[rows, width:]).astype(jnp.bfloat16)
        for send in lane_sends(buf, rows.start, rows, out, 1 - core, sem.at[number]):
            send.start()
            started.append(send)
    for send in started:
        send.wait()


def finish(modes, piece, total, before=None):
    ndof, depth = modes.shape
    width = piece.shape[1]
    out = jax.ShapeDtypeStruct((ndof, 2 * width), jnp.bfloat16)
    if before is None:
        kernel, operands = own_lane_kernel, [modes, piece, total]
        out_shape = [out, pltpu.VMEM((ndof - EARLY, width), jnp.bfloat16)]
        out_specs, alias = [ANY, VMEM], {}
        in_specs = [VMEM] * 3
        scratch = [pltpu.VMEM((EARLY, width), jnp.bfloat16), pltpu.SemaphoreType.DMA]
    else:
        kernel, operands = last_kernel, [modes, piece, total, before[1], before[0]]
        out_shape, out_specs, alias = out, ANY, {4: 0}
        in_specs = [VMEM] * 4 + [ANY]
        scratch = [
            pltpu.VMEM((ndof, width), jnp.bfloat16),
            pltpu.SemaphoreType.DMA((len(LAST_TILES) + 1,)),
        ]
    return pl.pallas_call(
        kernel,
        out_shape=out_shape,
        in_specs=in_specs,
        out_specs=out_specs,
        scratch_shapes=scratch,
        input_output_aliases=alias,
        compiler_params=params(GRANT),
        cost_estimate=pl.CostEstimate(
            flops=2 * ndof * width * depth, bytes_accessed=8 << 20, transcendentals=0
        ),
    )(*operands)


def shards(ritz_coefficients, mode_map, leaf_count, mode_blocks):
    *modes, pick = arrange(leaf_count, mode_map, exchange(mode_map, 1), mode_blocks)
    parts = lax.axis_size("sub") // 2
    width = ritz_coefficients.shape[1]
    lanes = [[2 * part + core for part in range(parts)] for core in range(2)]
    blocks = lax.all_to_all(
        ritz_coefficients.reshape(parts, -1, width),
        "sub",
        split_axis=0,
        concat_axis=0,
        tiled=True,
        axis_index_groups=lanes,
    )
    own, swap = place(pick, blocks, modes[2])

    def shares(low, high):
        at = LEAF + PAIR * LAID.index(low)
        return slice(at, LEAF + PAIR * (LAID.index(high) + 1))

    got = exchange(swap, 1)
    f = exchange(own[shares(5, 3)], 2)
    g = exchange(own[shares(5, 3)], 6)
    h = exchange(own[shares(4, 5)], 4)
    z = exchange(own[shares(4, 5)], 8)
    x = exchange(own[shares(5, 5)], 16)
    xz = exchange(own[shares(5, 5)], 24)
    total = product(modes[0], own, got)
    extra_f, extra_g = shares(2, 4), shares(4, 4)
    first, along_f, along_g, along_x = collect(
        [f, g, h, x, z, xz, own],
        [
            [(i, 0, None) for i in range(6)],
            [(4, 0, None), (5, 0, None), (6, extra_f.start, extra_f.stop)],
            [(4, 0, None), (5, 0, None), (0, PAIR, None), (6, extra_g.start, extra_g.stop)],
            [(0, 0, PAIR), (1, 0, PAIR), (2, PAIR, None)],
        ],
    )
    pieces = [
        exchange(along_f, 2),
        exchange(along_g, 6),
        exchange(h, 8),
        exchange(along_x, 16),
        exchange(h[PAIR:], 24),
    ]
    got = exchange(first, 1)
    total = product(modes[1], first, got, total)
    (last,) = collect(pieces, [[(i, 0, None) for i in range(5)]])
    got = exchange(last, 1)
    full = finish(modes[2], last, total)
    return finish(modes[2], got, total, full)


def solution(mesh):
    return jax.shard_map(
        shards,
        mesh=mesh,
        in_specs=(
            P("row", "sub"),
            P(("row", "sub"), None),
            P(("row", "sub")),
            P(("row", "sub"), None),
        ),
        out_specs=P(("row", "sub"), None),
        check_vma=False,
    )
```

```python
import functools

import jax
import jax.numpy as jnp
from jax import lax
from jax.experimental import pallas as pl
from jax.experimental.pallas import tpu as pltpu
from jax.sharding import PartitionSpec as P


SR = 16
LEAF = 48
PAIR = 2 * SR
AXES = ("row", "sub")


LAID = (1, 2, 4, 5, 3)
OWN = [(0, l) for l in LAID]
FIRST = (
    [(m, l) for m in (2, 6) for l in (5, 3)]
    + [(4, l) for l in (4, 5)]
    + [(16, 5)]
    + [(8, l) for l in (4, 5)]
    + [(24, 5)]
)
SECOND = (
    [(10, 4), (10, 5), (26, 5), (2, 2), (2, 4)]
    + [(14, 4), (14, 5), (30, 5), (4, 3), (6, 4)]
    + [(12, 4), (12, 5)]
    + [(18, 5), (22, 5), (20, 5)]
    + [(28, 5)]
)
CHUNKS = ([None] + OWN, FIRST, SECOND)
DEPTHS = (LEAF + PAIR * len(OWN), PAIR * len(FIRST), PAIR * len(SECOND))

FAR = 2

GRANT = 20 << 20
SMALL = 6 << 20
TILES = (1024, 1024)
LAST_TILES = (768, 768, 512)
EARLY = 256

VMEM = pl.BlockSpec(memory_space=pltpu.VMEM)
HBM = pl.BlockSpec(memory_space=pltpu.HBM)
ANY = pl.BlockSpec(memory_space=pl.ANY)


def in_hbm(value):
    return pltpu.with_memory_space_constraint(value, pltpu.HBM)


def exchange(value, mask):
    return lax.ppermute(value, AXES, [(i, i ^ mask) for i in range(128)])


def params(limit):
    return pltpu.CompilerParams(vmem_limit_bytes=limit)


def arrange_kernel(count, mine_hbm, theirs, blocks, *refs):
    outs, (pick, rows, mine, stage, sem) = refs[:-5], refs[-5:]
    own_map = pltpu.make_async_copy(mine_hbm, mine, sem.at[len(DEPTHS)])
    own_map.start()
    device = lax.axis_index("row") * lax.axis_size("sub") + lax.axis_index("sub")
    at, waits = 0, []
    for number, chunk in enumerate(CHUNKS):
        copies = []
        for share in chunk:
            if share is None:
                depth, start = LEAF, 0
            else:
                mask, level = share
                depth = PAIR
                peer = ((device ^ mask) & ((1 << level) - 1)) >> 1
                start = pl.multiple_of(SR * ((1 << level) + 1) + peer * PAIR, SR)
            copies.append(
                pltpu.make_async_copy(
                    blocks.at[pl.ds(start, depth), :], rows.at[at : at + depth, :], sem.at[number]
                )
            )
            at += depth
        for copy in copies:
            copy.start()
        waits.append(copies)
    own_map.wait()
    upper = lax.axis_index("sub") % 2 == 1
    local = lax.broadcasted_iota(jnp.int32, pick.shape[1:], 0)
    for core in range(2):
        slots = jnp.where(upper == (core == 1), mine[...], theirs[...])
        pick[core] = jnp.where(local == slots, 1.0, 0.0).astype(jnp.bfloat16)
    at = 0
    for number, copies in enumerate(waits):
        for copy in copies:
            copy.wait()
        depth = DEPTHS[number]
        value = rows[at : at + depth, :]
        if number == 0:
            row = lax.broadcasted_iota(jnp.int32, (LEAF, value.shape[1]), 0)
            leaf = jnp.where(row < count[0], value[:LEAF].astype(jnp.float32), 0.0)
            value = jnp.concatenate([leaf.astype(jnp.bfloat16), value[LEAF:]], axis=0)
        if number == FAR:
            stage[...] = value.T
            flush = pltpu.make_async_copy(stage, outs[number], sem.at[len(DEPTHS) + 1])
            flush.start()
        else:
            outs[number][...] = value.T
        at += depth
    flush.wait()


def arrange(leaf_count, mine, theirs, blocks):
    ndof = blocks.shape[1]
    kept = mine.shape[1]
    return pl.pallas_call(
        arrange_kernel,
        out_shape=[
            (pltpu.HBM if number == FAR else pltpu.VMEM)((ndof, depth), jnp.bfloat16)
            for number, depth in enumerate(DEPTHS)
        ]
        + [pltpu.VMEM((2, kept, kept), jnp.bfloat16)],
        in_specs=[
            pl.BlockSpec(memory_space=pltpu.SMEM),
            HBM,
            VMEM,
            HBM,
        ],
        out_specs=[HBM if number == FAR else VMEM for number in range(len(DEPTHS) + 1)],
        scratch_shapes=[
            pltpu.VMEM(blocks.shape, jnp.bfloat16),
            pltpu.VMEM(mine.shape, mine.dtype),
            pltpu.VMEM((ndof, DEPTHS[FAR]), jnp.bfloat16),
            pltpu.SemaphoreType.DMA((len(DEPTHS) + 2,)),
        ],
        compiler_params=params(GRANT),
        cost_estimate=pl.CostEstimate(flops=0, bytes_accessed=9 << 20, transcendentals=0),
        name="arrange",
    )(leaf_count, in_hbm(mine), theirs, in_hbm(blocks))


def place_kernel(pick, blocks, _, own, swap):
    upper = lax.axis_index("sub") % 2 == 1
    width = blocks.shape[2]
    kept = pick.shape[1]
    for part in range(blocks.shape[0]):
        columns = slice(part * width, (part + 1) * width)
        even, odd = (
            jnp.dot(
                pick[core],
                blocks[part, core * kept : (core + 1) * kept, :],
                preferred_element_type=jnp.float32,
            )
            for core in range(2)
        )
        own[:LEAF, columns] = jnp.where(upper, odd[:LEAF], even[:LEAF]).astype(jnp.bfloat16)
        swap[:LEAF, columns] = jnp.where(upper, even[:LEAF], odd[:LEAF]).astype(jnp.bfloat16)
        for place, level in enumerate(LAID):
            source = slice(LEAF + (level - 1) * SR, LEAF + level * SR)
            target = LEAF + place * PAIR
            for value in (even, odd):
                share = value[source].astype(jnp.bfloat16)
                own[target : target + SR, columns] = share
                swap[target : target + SR, columns] = share
                target += SR


def place(pick, blocks, after):
    parts, _, width = blocks.shape
    shape = pltpu.VMEM((DEPTHS[0], parts * width), jnp.bfloat16)
    return pl.pallas_call(
        place_kernel,
        out_shape=[shape, shape],
        in_specs=[VMEM, VMEM, ANY],
        out_specs=[VMEM, VMEM],
        compiler_params=params(SMALL),
        name="place",
    )(pick, blocks, after)


def cut(piece, start, stop):
    return (piece.shape[0] if stop is None else stop) - start


def collect_kernel(parts, *refs):
    count = len(refs) - len(parts)
    for part, out in zip(parts, refs[count:]):
        at = 0
        for index, start, stop in part:
            depth = cut(refs[index], start, stop)
            out[at : at + depth, :] = refs[index][start : start + depth, :]
            at += depth


def collect(pieces, parts):
    width = pieces[0].shape[1]
    return pl.pallas_call(
        functools.partial(collect_kernel, parts),
        out_shape=[
            pltpu.VMEM((sum(cut(pieces[i], a, b) for i, a, b in part), width), jnp.bfloat16)
            for part in parts
        ],
        in_specs=[VMEM] * len(pieces),
        out_specs=[VMEM] * len(parts),
        compiler_params=params(SMALL),
    )(*pieces)


def spans(heights):
    at = 0
    for height in heights:
        yield slice(at, at + height)
        at += height


def product_kernel(first, modes, own, got, *refs):
    total = refs[-1]
    piece = jnp.concatenate([own[...], got[...]], axis=1)
    for rows in spans(TILES):
        value = jnp.dot(modes[rows, :], piece, preferred_element_type=jnp.float32)
        if not first:
            value = value + refs[0][rows, :]
        total[rows, :] = value


def product(modes, own, got, total=None):
    ndof, depth = modes.shape
    width = 2 * own.shape[1]
    operands = [modes, own, got] + ([] if total is None else [total])
    return pl.pallas_call(
        functools.partial(product_kernel, total is None),
        out_shape=pltpu.VMEM((ndof, width), jnp.float32),
        in_specs=[VMEM] * len(operands),
        out_specs=VMEM,
        input_output_aliases={} if total is None else {3: 0},
        compiler_params=params(GRANT),
        cost_estimate=pl.CostEstimate(
            flops=2 * ndof * width * depth, bytes_accessed=8 << 20, transcendentals=0
        ),
    )(*operands)


def lane_sends(source, at, rows, out, core, sem):
    depth = rows.stop - rows.start
    return [
        pltpu.make_async_copy(
            source.at[at : at + depth, part * 128 : (part + 1) * 128],
            out.at[rows, pl.ds(pl.multiple_of((2 * part + core) * 128, 128), 128)],
            sem,
        )
        for part in range(source.shape[1] // 128)
    ]


def own_lane_kernel(modes, piece, total, out, rest, buf, sem):
    core = lax.axis_index("sub") % 2
    width = piece.shape[1]
    early, late = spans((buf.shape[0], rest.shape[0]))
    sends = []
    for rows, target in ((early, buf), (late, rest)):
        value = jnp.dot(modes[rows, :], piece[...], preferred_element_type=jnp.float32)
        target[...] = (value + total[rows, :width]).astype(jnp.bfloat16)
        if target is buf:
            sends = lane_sends(buf, 0, rows, out, core, sem)
            for send in sends:
                send.start()
    for send in sends:
        send.wait()


def last_kernel(modes, piece, total, rest, _, out, buf, sem):
    core = lax.axis_index("sub") % 2
    width = piece.shape[1]
    late = slice(modes.shape[0] - rest.shape[0], modes.shape[0])
    started = lane_sends(rest, 0, late, out, core, sem.at[len(LAST_TILES)])
    for send in started:
        send.start()
    for number, rows in enumerate(spans(LAST_TILES)):
        value = jnp.dot(modes[rows, :], piece[...], preferred_element_type=jnp.float32)
        buf[rows, :] = (value + total[rows, width:]).astype(jnp.bfloat16)
        for send in lane_sends(buf, rows.start, rows, out, 1 - core, sem.at[number]):
            send.start()
            started.append(send)
    for send in started:
        send.wait()


def finish(modes, piece, total, before=None):
    ndof, depth = modes.shape
    width = piece.shape[1]
    out = jax.ShapeDtypeStruct((ndof, 2 * width), jnp.bfloat16)
    if before is None:
        kernel, operands = own_lane_kernel, [modes, piece, total]
        out_shape = [out, pltpu.VMEM((ndof - EARLY, width), jnp.bfloat16)]
        out_specs, alias = [ANY, VMEM], {}
        in_specs = [VMEM] * 3
        scratch = [pltpu.VMEM((EARLY, width), jnp.bfloat16), pltpu.SemaphoreType.DMA]
    else:
        kernel, operands = last_kernel, [modes, piece, total, before[1], before[0]]
        out_shape, out_specs, alias = out, ANY, {4: 0}
        in_specs = [VMEM] * 4 + [ANY]
        scratch = [
            pltpu.VMEM((ndof, width), jnp.bfloat16),
            pltpu.SemaphoreType.DMA((len(LAST_TILES) + 1,)),
        ]
    return pl.pallas_call(
        kernel,
        out_shape=out_shape,
        in_specs=in_specs,
        out_specs=out_specs,
        scratch_shapes=scratch,
        input_output_aliases=alias,
        compiler_params=params(GRANT),
        cost_estimate=pl.CostEstimate(
            flops=2 * ndof * width * depth, bytes_accessed=8 << 20, transcendentals=0
        ),
    )(*operands)


def shards(ritz_coefficients, mode_map, leaf_count, mode_blocks):
    *modes, pick = arrange(leaf_count, mode_map, exchange(mode_map, 1), mode_blocks)
    parts = lax.axis_size("sub") // 2
    width = ritz_coefficients.shape[1]
    lanes = [[2 * part + core for part in range(parts)] for core in range(2)]
    blocks = lax.all_to_all(
        ritz_coefficients.reshape(parts, -1, width),
        "sub",
        split_axis=0,
        concat_axis=0,
        tiled=True,
        axis_index_groups=lanes,
    )
    own, swap = place(pick, blocks, modes[0])

    def shares(low, high):
        at = LEAF + PAIR * LAID.index(low)
        return slice(at, LEAF + PAIR * (LAID.index(high) + 1))

    got = exchange(swap, 1)
    f = exchange(own[shares(5, 3)], 2)
    g = exchange(own[shares(5, 3)], 6)
    h = exchange(own[shares(4, 5)], 4)
    z = exchange(own[shares(4, 5)], 8)
    x = exchange(own[shares(5, 5)], 16)
    xz = exchange(own[shares(5, 5)], 24)
    total = product(modes[0], own, got)
    extra_f, extra_g = shares(2, 4), shares(4, 4)
    first, along_f, along_g, along_x = collect(
        [f, g, h, x, z, xz, own],
        [
            [(i, 0, None) for i in range(6)],
            [(4, 0, None), (5, 0, None), (6, extra_f.start, extra_f.stop)],
            [(4, 0, None), (5, 0, None), (0, PAIR, None), (6, extra_g.start, extra_g.stop)],
            [(0, 0, PAIR), (1, 0, PAIR), (2, PAIR, None)],
        ],
    )
    pieces = [
        exchange(along_f, 2),
        exchange(along_g, 6),
        exchange(h, 8),
        exchange(along_x, 16),
        exchange(h[PAIR:], 24),
    ]
    got = exchange(first, 1)
    total = product(modes[1], first, got, total)
    (last,) = collect(pieces, [[(i, 0, None) for i in range(5)]])
    got = exchange(last, 1)
    full = finish(modes[2], last, total)
    return finish(modes[2], got, total, full)


def solution(mesh):
    return jax.shard_map(
        shards,
        mesh=mesh,
        in_specs=(
            P("row", "sub"),
            P(("row", "sub"), None),
            P(("row", "sub")),
            P(("row", "sub"), None),
        ),
        out_specs=P(("row", "sub"), None),
        check_vma=False,
    )
```
